32 devices in a mesh: pair: 4 (over x, core), tile: 8 (over z, y).
Axes of the slice: x: 2, y: 2, z: 4, core: 2. Of those that a mesh axis runs over, the one named last changes fastest.
Arguments:
- interferograms: float32 [1024, 64, 128], P(('pair', 'tile')), may hold values from -6 to 6
- coherence: int32 [2, 64, 128], P(None, 'pair', 'tile'), may hold values 0 or 1
- epochs: int32 [1024, 2], replicated, may hold values from 0 to 399, as said below
- track: int32 [1024], replicated, may hold values from 0 to 1, as said below
Outputs:
- displacement: float32 [2, 400, 64, 128], P(None, None, 'pair', 'tile')
The draws below stay inside these ranges and needn't reach their ends.
Inputs may be any that keep to these rules, and one draw needn't show every extreme that they name: Each row names an earlier and a later epoch, 1 to 12 epochs apart; row 0 starts at epoch 0 and row 1023 ends at epoch 400 - 1. `track`: exactly 576 entries are 0.
All inputs are finite; a program needn't handle non-finite values. No bound on the sum of `coherence` on one device may be relied on, other than what follows from the above.
Results may differ from the reference program's by a relative error of at most 0.0013.
Values may be sent and summed in bfloat16 or wider, within the bound.
A program may use at most 128 MiB of HBM per device.

```python
import jax
import jax.numpy as jnp
from jax import lax

NPAIR = 1024
ASC = 576
NEPOCH = 400
PATCH = 16
RADIUS = 4
ROUNDS = 4
CG_STEPS = 2
NROW = 64
NCOL = 128
N_PAIR = 4
N_TILE = 8


def draw_epochs(key, part):
    base_key = jax.random.fold_in(key, 11)
    gap_key, start_key = jax.random.split(base_key)
    epoch_gap = jax.random.randint(gap_key, (NPAIR,), 1, 13)
    first_epoch = jax.random.randint(start_key, (NPAIR,), 0, NEPOCH - epoch_gap)
    first_epoch = first_epoch.at[0].set(0)
    first_epoch = first_epoch.at[NPAIR - 1].set(NEPOCH - 1 - epoch_gap[NPAIR - 1])
    return jnp.stack([first_epoch, first_epoch + epoch_gap], axis=1).astype(jnp.int32)


def draw_track(key, part):
    shuffled = jax.random.permutation(jax.random.fold_in(key, 5), NPAIR)
    return (shuffled >= ASC).astype(jnp.int32)


def plant(values, rng, low, high):
    index_at = [jax.random.randint(jax.random.fold_in(rng, axis), (), 0, length) for axis, length in enumerate(values.shape)]
    widest = values.shape.index(max(values.shape))
    next_to = index_at[:widest] + [(index_at[widest] + 1) % values.shape[widest]] + index_at[widest + 1:]
    return values.at[tuple(index_at)].set(low).at[tuple(next_to)].set(high)


def level_of(rng, shape, pieces, low, top_value):
    level = 1.0
    for dim, shards_of in pieces:
        draws = jax.random.uniform(jax.random.fold_in(jax.random.fold_in(rng, 6), dim), (shards_of,), jnp.float32, low / len(pieces), top_value / len(pieces))
        level = level * jnp.repeat(jnp.exp(draws), shape[dim] // shards_of).reshape((-1,) + (1,) * (len(shape) - 1 - dim))
    return level


def gaussian(own_key, extent, deviation, limit, cuts=(), held_as=jnp.bfloat16):
    factor_of = level_of(own_key, extent, cuts, -0.22, 0.18) if cuts else 1.0
    entries = jax.random.normal(own_key, extent, jnp.float32) * deviation * factor_of
    return jnp.minimum(jnp.maximum(entries, -limit), limit).astype(held_as)


def setup_inputs(seed: int = 0) -> dict:
    seeds = jax.random.split(jax.random.key(seed), 5)
    return {
        "interferograms": gaussian(seeds[0], (NPAIR, NROW, NCOL), 1.0, 6.0, ((0, 32),), jnp.float32),
        "coherence": plant((jax.random.randint(seeds[1], (2, NROW, NCOL), 0, 4) < 3).astype(jnp.int32), jax.random.fold_in(seeds[1], 1), 0, 1),
        "epochs": draw_epochs(jax.random.fold_in(seeds[4], 71), 0),
        "track": draw_track(jax.random.fold_in(seeds[4], 71), 0),
    }


ALPHA_EXP = 0.5
HUBER_EDGE = 0.5
TIKHONOV = 1.0
EPSILON = 1e-06

def box_mean(field_in):
    total_sum = jnp.zeros_like(field_in)
    for shift_row in (-1, 0, 1):
        for shift_col in (-1, 0, 1):
            total_sum = total_sum + jnp.roll(field_in, (shift_row, shift_col), axis=(-2, -1))
    return total_sum / 9.0

def goldstein_ref(patches):
    spectrum = jnp.fft.fft2(patches)
    magnitude = jnp.sqrt(jnp.real(spectrum) ** 2 + jnp.imag(spectrum) ** 2 + 1.0)
    weights = box_mean(magnitude) ** ALPHA_EXP
    restored = jnp.real(jnp.fft.ifft2(spectrum * weights))
    return restored / lax.optimization_barrier(jnp.mean(weights, axis=(-2, -1), keepdims=True))

def design_matrix(epochs, track):
    earlier_epoch = epochs[:, 0].astype(jnp.int32)
    later_epoch = epochs[:, 1].astype(jnp.int32)
    ascending = track == 0
    up_coef = jnp.where(ascending, 0.8, 0.75).astype(jnp.float32)
    east_coef = jnp.where(ascending, -0.6, 0.66).astype(jnp.float32)
    epoch_ids = jnp.arange(NEPOCH, dtype=jnp.int32)
    change = (later_epoch[:, None] == epoch_ids[None, :]).astype(jnp.float32) - (earlier_epoch[:, None] == epoch_ids[None, :]).astype(jnp.float32)
    return jnp.concatenate([up_coef[:, None] * change, east_coef[:, None] * change], axis=1)

def apply_design(field_in, matrix):
    return jnp.dot(matrix, field_in, precision=lax.Precision.HIGHEST, preferred_element_type=jnp.float32)

def apply_transpose(pair_values, matrix):
    return lax.dot_general(matrix, pair_values, (((0,), (0,)), ((), ())), precision=lax.Precision.HIGHEST, preferred_element_type=jnp.float32)

def gauss_taps():
    offsets = jnp.arange(-RADIUS, RADIUS + 1).astype(jnp.float32)
    raw_taps = jnp.exp(-offsets * offsets / 8.0)
    return raw_taps / jnp.sum(raw_taps)

def smooth_padded(padded, rows_out, cols_out):
    tap_values = gauss_taps()
    along_rows = tap_values[0] * padded[:, 0:rows_out, :]
    for tap_index in range(1, 2 * RADIUS + 1):
        along_rows = along_rows + tap_values[tap_index] * padded[:, tap_index:tap_index + rows_out, :]
    result_sum = tap_values[0] * along_rows[:, :, 0:cols_out]
    for tap_index in range(1, 2 * RADIUS + 1):
        result_sum = result_sum + tap_values[tap_index] * along_rows[:, :, tap_index:tap_index + cols_out]
    return result_sum

def invert(observed, mask_cells, epochs, track, smoother):
    matrix = design_matrix(epochs, track)
    measured = observed.astype(jnp.float32)
    pair_mask = jnp.where((track == 0)[:, None], mask_cells[0][None, :], mask_cells[1][None, :])
    solution = jnp.zeros((2 * NEPOCH, measured.shape[1]), jnp.float32)
    for outer_no in range(ROUNDS):
        misfit = measured - apply_design(solution, matrix)
        weights = pair_mask * HUBER_EDGE / jnp.maximum(jnp.abs(misfit), HUBER_EDGE)

        def normal_apply(field_in):
            return apply_transpose(weights * apply_design(field_in, matrix), matrix) + TIKHONOV * field_in
        residual = apply_transpose(weights * measured, matrix) - normal_apply(solution)
        direction = residual
        norm_now = lax.optimization_barrier(jnp.sum(residual * residual, axis=0))
        for inner_no in range(CG_STEPS):
            mapped = normal_apply(direction)
            step_len = norm_now / (lax.optimization_barrier(jnp.sum(direction * mapped, axis=0)) + EPSILON)
            solution = solution + step_len * direction
            residual = residual - step_len * mapped
            if inner_no + 1 < CG_STEPS:
                norm_next = lax.optimization_barrier(jnp.sum(residual * residual, axis=0))
                direction = residual + norm_next / (norm_now + EPSILON) * direction
                norm_now = norm_next
        solution = smoother(solution)
    return solution

def reference(interferograms, coherence, epochs, track):

    def filter_one(image_in):
        patches = image_in.reshape(N_PAIR, PATCH, N_TILE, PATCH).transpose(0, 2, 1, 3)
        restored = goldstein_ref(patches)
        return restored.transpose(0, 2, 1, 3).reshape(NROW, NCOL)
    cleaned = lax.map(filter_one, interferograms).astype(jnp.bfloat16)
    observed = cleaned.reshape(NPAIR, NROW * NCOL)
    mask_cells = coherence.reshape(2, NROW * NCOL).astype(jnp.float32)

    def smoother(field_in):
        grid_form = field_in.reshape(-1, NROW, NCOL)
        padded = jnp.pad(grid_form, ((0, 0), (RADIUS, RADIUS), (RADIUS, RADIUS)))
        return smooth_padded(padded, NROW, NCOL).reshape(field_in.shape[0], -1)
    solution = invert(observed, mask_cells, epochs, track, smoother)
    return solution.reshape(2, NEPOCH, NROW, NCOL)
```

```python
import functools
import math

import jax
import jax.numpy as jnp
import numpy as np
from jax import lax
from jax.experimental import pallas as pl
from jax.experimental.pallas import tpu as pltpu
from jax.sharding import PartitionSpec as P

NEPOCH = 400
ASC = 576
RADIUS = 4
ROUNDS = 4
CG_STEPS = 2


HUBER_EDGE = 0.5
TIKHONOV = 1.0
EPSILON = 1e-06


UP_COEF = (0.8, 0.75)
EAST_COEF = (-0.6, 0.66)
MESH = pl.DeviceIdType.MESH
WHOLE = pl.BlockSpec(memory_space=pltpu.VMEM)


def mm(left, right):
    return jnp.dot(left, right, preferred_element_type=jnp.float32)


def mm_nt(left, right):
    return lax.dot_general(
        left, right, (((1,), (1,)), ((), ())), preferred_element_type=jnp.float32
    )


def mm_tn(left, right):
    return lax.dot_general(
        left, right, (((0,), (0,)), ((), ())), preferred_element_type=jnp.float32
    )


def halves(value):
    high = value.astype(jnp.bfloat16)
    return high, (value - high.astype(jnp.float32)).astype(jnp.bfloat16)


def spectral_tables(side):
    cells = side * side
    index = np.arange(cells)
    row, col = index // side, index % side
    phase = (row[:, None] * row[None, :] + col[:, None] * col[None, :]) % side
    angle = phase * (2.0 * math.pi / side)

    def split(value):
        high = value.astype(np.float32).astype(jnp.bfloat16)
        return high, (value - high.astype(np.float64)).astype(jnp.bfloat16)

    near_row = (row[:, None] - row[None, :] + 1) % side <= 2
    near_col = (col[:, None] - col[None, :] + 1) % side <= 2
    box = (near_row & near_col).astype(np.float32).astype(jnp.bfloat16)
    turn = np.concatenate([np.cos(angle), -np.sin(angle)], axis=0)
    return [jnp.asarray(t) for t in (*split(turn), box)]


def filter_kernel(local, side, x_ref, turn_hi, turn_lo, box_ref, out_ref, cells_ref):
    full_rows = x_ref.shape[1] // local
    full_cols = x_ref.shape[0] * 128
    cells = side * side
    bands = full_rows // side
    group = bands * local
    tiles = full_cols // side
    per_block = 128 // side
    for line in range(side):
        for block in range(full_cols // 128):
            stacked = jnp.concatenate(
                [
                    x_ref[block, pl.ds(band * side + line, local, stride=full_rows), :]
                    for band in range(bands)
                ],
                axis=0,
            )
            flipped = stacked.T
            for inner in range(per_block):
                tile = block * per_block + inner
                cells_ref[
                    line * side : (line + 1) * side, tile * group : (tile + 1) * group
                ] = flipped[inner * side : (inner + 1) * side]
    step = 2
    for first in range(0, tiles, step):
        span = slice(first * group, (first + step) * group)
        high, low = halves(cells_ref[:, span])
        spectrum = mm(turn_hi[...], high) + mm(turn_lo[...], high) + mm(turn_hi[...], low)
        real, imag = spectrum[:cells], spectrum[cells:]
        magnitude = jnp.sqrt(real * real + imag * imag + 1.0)
        high, low = halves(magnitude)
        weight = jnp.sqrt((mm(box_ref[...], high) + mm(box_ref[...], low)) / 9.0)
        mean = jnp.sum(weight, axis=0, keepdims=True) / cells
        scaled = jnp.concatenate([real * weight, imag * weight], axis=0) / (cells * mean)
        high, low = halves(scaled)
        for inner in range(step):
            part = slice(inner * group, (inner + 1) * group)
            restored = (
                mm_tn(high[:, part], turn_hi[...])
                + mm_tn(low[:, part], turn_hi[...])
                + mm_tn(high[:, part], turn_lo[...])
            ).astype(jnp.bfloat16)
            for band in range(bands):
                out_ref[band * tiles + first + inner] = restored[
                    band * local : (band + 1) * local
                ]


def filtered(interferograms, rows_split, side):
    local, full_rows, full_cols = interferograms.shape
    cells = side * side
    tiles = full_cols // side
    tables = spectral_tables(side)
    blocks = interferograms.reshape(local * full_rows, full_cols // 128, 128)
    return pl.pallas_call(
        functools.partial(filter_kernel, local, side),
        out_shape=jax.ShapeDtypeStruct((rows_split * tiles, local, cells), jnp.bfloat16),
        in_specs=[WHOLE] * 4,
        out_specs=WHOLE,
        scratch_shapes=[pltpu.VMEM((cells, tiles * rows_split * local), jnp.float32)],
        compiler_params=pltpu.CompilerParams(vmem_limit_bytes=40 * 1024 * 1024),
        name="filter",
    )(blocks.transpose(1, 0, 2), *tables)


def prepare_kernel(epochs_ref, track_ref, c0_ref, c1_ref, ct0_ref, ct1_ref, perm_ref):
    pairs = track_ref.shape[1]
    ascending = (track_ref[...] == 0).astype(jnp.float32)
    one = jnp.broadcast_to(ascending, (8, pairs)).astype(jnp.bfloat16)
    row_id = lax.broadcasted_iota(jnp.int32, (pairs, pairs), 0)
    col_id = lax.broadcasted_iota(jnp.int32, (pairs, pairs), 1)
    upto = (row_id <= col_id).astype(jnp.float32).astype(jnp.bfloat16)
    count = mm(one, upto)[0:1].astype(jnp.int32)
    place = lax.broadcasted_iota(jnp.int32, (1, pairs), 1)
    position = jnp.where(track_ref[...] == 0, count - 1, ASC + place - count)
    perm = (row_id == position).astype(jnp.float32).astype(jnp.bfloat16)
    perm_ref[...] = perm
    epoch_id = lax.broadcasted_iota(jnp.int32, (NEPOCH, pairs), 0)
    change = (epoch_id == epochs_ref[1:2, :]).astype(jnp.float32) - (
        epoch_id == epochs_ref[0:1, :]
    ).astype(jnp.float32)
    change = change.astype(jnp.bfloat16)
    c0_ref[...] = mm_nt(perm[:ASC], change).astype(jnp.bfloat16)
    c1_ref[...] = mm_nt(perm[ASC:], change).astype(jnp.bfloat16)
    ct0_ref[...] = mm_nt(change, perm[:ASC]).astype(jnp.bfloat16)
    ct1_ref[...] = mm_nt(change, perm[ASC:]).astype(jnp.bfloat16)


def prepare(epochs, track):
    pairs = track.shape[0]
    rest = pairs - ASC
    shapes = ((ASC, NEPOCH), (rest, NEPOCH), (NEPOCH, ASC), (NEPOCH, rest), (pairs, pairs))
    return pl.pallas_call(
        prepare_kernel,
        out_shape=[jax.ShapeDtypeStruct(s, jnp.bfloat16) for s in shapes],
        in_specs=[WHOLE] * 2,
        out_specs=[WHOLE] * 5,
        cost_estimate=pl.CostEstimate(
            flops=6 * pairs * pairs * NEPOCH, bytes_accessed=8 * pairs * pairs, transcendentals=0
        ),
        name="prepare",
    )(epochs.T, track[None, :])


def smoothing_tables(side):
    cells = side * side
    offsets = jnp.arange(-RADIUS, RADIUS + 1).astype(jnp.float32)
    total = jnp.sum(jnp.exp(-offsets * offsets / 8.0))

    def tap(distance):
        near = jnp.abs(distance) <= RADIUS
        value = jnp.exp(-(distance * distance).astype(jnp.float32) / 8.0) / total
        return jnp.where(near, value, 0.0)

    cell = jnp.arange(cells, dtype=jnp.int32)
    row, col = cell // side, cell % side
    strip = jnp.arange(2 * side * RADIUS, dtype=jnp.int32)
    half, inner = strip // (side * RADIUS), strip % (side * RADIUS)
    tables, picks = [], []
    for mine, other, s_mine, s_other in (
        (row, col, inner // side, inner % side),
        (col, row, inner % RADIUS, inner // RADIUS),
    ):
        same = other[:, None] == other[None, :]
        tables.append(jnp.where(same, tap(mine[:, None] - mine[None, :]), 0.0))
        lines = s_other[:, None] == other[None, :]
        for shift in (-RADIUS, side):
            value = jnp.where(lines, tap(s_mine[:, None] + shift - mine[None, :]), 0.0)
            for part in (0, 1):
                tables.append(jnp.where((half == part)[:, None], value, 0.0))
        for first in (0, side - RADIUS):
            hit = (other[:, None] == s_other[None, :]) & (
                mine[:, None] == s_mine[None, :] + first
            )
            for part in (0, 1):
                picks.append((hit & (half == part)[None, :]).astype(jnp.bfloat16))
    own = jnp.stack([tables[0], tables[5]])
    strips = jnp.stack(tables[1:5] + tables[6:10])

    def split(value):
        high = lax.reduce_precision(value, 8, 7)
        return high.astype(jnp.bfloat16), (value - high).astype(jnp.bfloat16)

    return split(own) + split(strips) + (jnp.stack(picks),)


def invert_kernel(
    obs_ref, mask_ref, c0_ref, c1_ref, ct0_ref, ct1_ref, perm_ref,
    own_hi, own_lo, strip_hi, strip_lo, pick_ref,
    out_ref, meas_ref, weight_ref, send_buf, recv_buf, send_sem, recv_sem,
):
    design = (c0_ref, c1_ref)
    transposed = (ct0_ref, ct1_ref)
    spans = (slice(0, ASC), slice(ASC, obs_ref.shape[0]))
    me = {name: lax.axis_index(name) for name in ("pair", "tile")}
    size = {name: lax.axis_size(name) for name in ("pair", "tile")}
    axes = ("pair", "tile")

    def there(axis, step):
        return {"pair": me["pair"], "tile": me["tile"], axis: me[axis] + step}

    def target(axis, step):
        where = there(axis, step)
        return (where["pair"], where["tile"])

    def has(axis, step):
        return me[axis] > 0 if step < 0 else me[axis] < size[axis] - 1

    recv_buf[...] = jnp.zeros_like(recv_buf)
    barrier = pltpu.get_barrier_semaphore()
    for axis in axes:
        for step in (-1, 1):

            @pl.when(has(axis, step))
            def _():
                pl.semaphore_signal(
                    barrier, inc=1, device_id=target(axis, step), device_id_type=MESH
                )

    meas_ref[...] = mm(perm_ref[...], obs_ref[...])
    out_ref[...] = jnp.zeros_like(out_ref)

    peers = sum(
        jnp.where(has(axis, step), 1, 0) for axis in axes for step in (-1, 1)
    )
    pl.semaphore_wait(barrier, peers)

    def forward(field, track, passes):
        mixed = UP_COEF[track] * field[:NEPOCH] + EAST_COEF[track] * field[NEPOCH:]
        high, low = halves(mixed)
        result = mm(design[track][...], high)
        if passes > 1:
            result = result + mm(design[track][...], low)
        return result

    def backward(parts):
        sums = []
        for track in (0, 1):
            high, low = halves(parts[track])
            sums.append(mm(transposed[track][...], high) + mm(transposed[track][...], low))
        return jnp.concatenate(
            [
                UP_COEF[0] * sums[0] + UP_COEF[1] * sums[1],
                EAST_COEF[0] * sums[0] + EAST_COEF[1] * sums[1],
            ],
            axis=0,
        )

    def total(value):
        return jnp.sum(value, axis=0, keepdims=True)

    def exchange(turn, which, field_hi):
        axis = axes[which]
        copies = []
        for side, step in ((0, -1), (1, 1)):
            slot = 2 * which + side
            edge = mm(field_hi[:NEPOCH], pick_ref[2 * slot]) + mm(
                field_hi[NEPOCH:], pick_ref[2 * slot + 1]
            )
            send_buf[turn, slot] = edge.astype(jnp.bfloat16)
            landing = 2 * which + 1 - side
            copy = pltpu.make_async_remote_copy(
                src_ref=send_buf.at[turn, slot],
                dst_ref=recv_buf.at[turn, landing],
                send_sem=send_sem.at[turn, slot],
                recv_sem=recv_sem.at[turn, landing],
                device_id=target(axis, step),
                device_id_type=MESH,
            )

            @pl.when(has(axis, step))
            def _():
                copy.start()

            copies.append((copy, axis, step, slot))
        return copies

    def smooth_own(which, high, low):
        return mm(high, own_hi[which]) + mm(high, own_lo[which]) + mm(low, own_hi[which])

    def finish(turn, which, copies):
        for copy, axis, step, slot in copies:
            incoming = pltpu.make_async_remote_copy(
                src_ref=send_buf.at[turn, slot],
                dst_ref=recv_buf.at[turn, slot],
                send_sem=send_sem.at[turn, slot],
                recv_sem=recv_sem.at[turn, slot],
                device_id=target(axis, step),
                device_id_type=MESH,
            )

            @pl.when(has(axis, step))
            def _():
                copy.wait_send()
                incoming.wait_recv()

        parts = []
        for part in (0, 1):
            value = 0.0
            for side in (0, 1):
                slot = 2 * which + side
                index = 2 * slot + part
                edge = recv_buf[turn, slot]
                value = value + mm(edge, strip_hi[index]) + mm(edge, strip_lo[index])
            parts.append(value)
        return jnp.concatenate(parts, axis=0)

    def one_round(turn, carry):
        solution = out_ref[...]
        pulls = []
        for track in (0, 1):
            misfit = meas_ref[spans[track]] - forward(solution, track, 2)
            weight = mask_ref[track : track + 1] * HUBER_EDGE / jnp.maximum(
                jnp.abs(misfit), HUBER_EDGE
            )
            weight_ref[spans[track]] = weight
            pulls.append(weight * misfit)
        residual = backward(pulls) - TIKHONOV * solution
        norm = total(residual * residual)
        pulls, curve = [], TIKHONOV * norm
        for track in (0, 1):
            image = forward(residual, track, 2)
            pull = weight_ref[spans[track]] * image
            curve = curve + total(pull * image)
            pulls.append(pull)
        step_len = norm / (curve + EPSILON)
        solution = solution + step_len * residual
        after = residual - step_len * (backward(pulls) + TIKHONOV * residual)
        norm_next = total(after * after)
        direction = after + norm_next / (norm + EPSILON) * residual
        curve = TIKHONOV * total(direction * direction)
        for track in (0, 1):
            image = forward(direction, track, 1)
            curve = curve + total(weight_ref[spans[track]] * image * image)
        solution = solution + norm_next / (curve + EPSILON) * direction
        for which in (0, 1):
            high, low = halves(solution)
            copies = exchange(turn, which, high)
            solution = smooth_own(which, high, low)
            solution = solution + finish(turn, which, copies)
        out_ref[...] = solution
        return carry

    lax.fori_loop(0, ROUNDS, one_round, 0)


def invert(observed, mask_cells, epochs, track, side):
    pairs, cells = observed.shape
    strip = 2 * side * RADIUS
    tables = smoothing_tables(side)
    return pl.pallas_call(
        invert_kernel,
        out_shape=jax.ShapeDtypeStruct((2 * NEPOCH, cells), jnp.float32),
        in_specs=[WHOLE] * 12,
        out_specs=WHOLE,
        scratch_shapes=[
            pltpu.VMEM((pairs, cells), jnp.float32),
            pltpu.VMEM((pairs, cells), jnp.float32),
            pltpu.VMEM((ROUNDS, 4, NEPOCH, strip), jnp.bfloat16),
            pltpu.VMEM((ROUNDS, 4, NEPOCH, strip), jnp.bfloat16),
            pltpu.SemaphoreType.DMA((ROUNDS, 4)),
            pltpu.SemaphoreType.DMA((ROUNDS, 4)),
        ],
        compiler_params=pltpu.CompilerParams(
            collective_id=0, has_side_effects=True, vmem_limit_bytes=60 * 1024 * 1024
        ),
        name="invert",
    )(observed, mask_cells, *prepare(epochs, track), *tables)


def per_device(interferograms, coherence, epochs, track):
    rows_split = lax.axis_size("pair")
    local_pairs, full_rows, full_cols = interferograms.shape
    patch_len = full_rows // rows_split
    cell_count = patch_len * patch_len
    cleaned = filtered(interferograms, rows_split, patch_len)
    received = lax.all_to_all(
        cleaned,
        ("pair", "tile"),
        split_axis=0,
        concat_axis=0,
        tiled=True,
    )
    observed = received.reshape(-1, cell_count)
    mask_cells = coherence.reshape(2, cell_count).astype(jnp.float32)

    solution = invert(observed, mask_cells, epochs, track, patch_len)
    return solution.reshape(2, NEPOCH, patch_len, patch_len)


def solution(mesh):
    placed = (P(("pair", "tile"), None, None), P(None, "pair", "tile"), P(), P())
    return jax.shard_map(
        per_device,
        mesh=mesh,
        in_specs=placed,
        out_specs=P(None, None, "pair", "tile"),
        check_vma=False,
    )
```

```python
import functools
import math

import jax
import jax.numpy as jnp
import numpy as np
from jax import lax
from jax.experimental import pallas as pl
from jax.experimental.pallas import tpu as pltpu
from jax.sharding import PartitionSpec as P

NEPOCH = 400
ASC = 576
RADIUS = 4
ROUNDS = 4
CG_STEPS = 2


HUBER_EDGE = 0.5
TIKHONOV = 1.0
EPSILON = 1e-06


UP_COEF = (0.8, 0.75)
EAST_COEF = (-0.6, 0.66)
MESH = pl.DeviceIdType.MESH
WHOLE = pl.BlockSpec(memory_space=pltpu.VMEM)


def mm(left, right):
    return jnp.dot(left, right, preferred_element_type=jnp.float32)


def mm_nt(left, right):
    return lax.dot_general(
        left, right, (((1,), (1,)), ((), ())), preferred_element_type=jnp.float32
    )


def mm_tn(left, right):
    return lax.dot_general(
        left, right, (((0,), (0,)), ((), ())), preferred_element_type=jnp.float32
    )


def halves(value):
    high = value.astype(jnp.bfloat16)
    return high, (value - high.astype(jnp.float32)).astype(jnp.bfloat16)


def split_table(value):
    high = value.astype(np.float32).astype(jnp.bfloat16)
    return high, (value - high.astype(np.float64)).astype(jnp.bfloat16)


def spectral_tables(side):
    cells = side * side
    index = np.arange(cells)
    row, col = index // side, index % side
    phase = (row[:, None] * row[None, :] + col[:, None] * col[None, :]) % side
    angle = phase * (2.0 * math.pi / side)

    near_row = (row[:, None] - row[None, :] + 1) % side <= 2
    near_col = (col[:, None] - col[None, :] + 1) % side <= 2
    box = (near_row & near_col).astype(np.float32).astype(jnp.bfloat16)
    turn = np.concatenate([np.cos(angle), -np.sin(angle)], axis=0)
    return [jnp.asarray(t) for t in (*split_table(turn), box)]


def filter_kernel(
    local, side, x_hbm, hi_hbm, lo_hbm, box_hbm, out_ref,
    cells_ref, x_ref, turn_hi, turn_lo, box_ref, sems,
):
    fetches = [
        pltpu.make_async_copy(source, held, sems.at[number])
        for number, (source, held) in enumerate(
            ((x_hbm, x_ref), (hi_hbm, turn_hi), (lo_hbm, turn_lo), (box_hbm, box_ref))
        )
    ]
    for fetch in fetches:
        fetch.start()
    fetches[0].wait()
    full_rows = x_ref.shape[1] // local
    full_cols = x_ref.shape[0] * 128
    cells = side * side
    bands = full_rows // side
    group = bands * local
    tiles = full_cols // side
    per_block = 128 // side
    for line in range(side):
        for block in range(full_cols // 128):
            stacked = jnp.concatenate(
                [
                    x_ref[block, pl.ds(band * side + line, local, stride=full_rows), :]
                    for band in range(bands)
                ],
                axis=0,
            )
            flipped = stacked.T
            for inner in range(per_block):
                tile = block * per_block + inner
                cells_ref[
                    line * side : (line + 1) * side, tile * group : (tile + 1) * group
                ] = flipped[inner * side : (inner + 1) * side]
    for fetch in fetches[1:]:
        fetch.wait()
    step = 2
    for first in range(0, tiles, step):
        span = slice(first * group, (first + step) * group)
        high, low = halves(cells_ref[:, span])
        spectrum = mm(turn_hi[...], high) + mm(turn_lo[...], high) + mm(turn_hi[...], low)
        real, imag = spectrum[:cells], spectrum[cells:]
        magnitude = jnp.sqrt(real * real + imag * imag + 1.0)
        high, low = halves(magnitude)
        weight = jnp.sqrt((mm(box_ref[...], high) + mm(box_ref[...], low)) / 9.0)
        mean = jnp.sum(weight, axis=0, keepdims=True) / cells
        scaled = jnp.concatenate([real * weight, imag * weight], axis=0) / (cells * mean)
        high, low = halves(scaled)
        for inner in range(step):
            part = slice(inner * group, (inner + 1) * group)
            restored = (
                mm_tn(high[:, part], turn_hi[...])
                + mm_tn(low[:, part], turn_hi[...])
                + mm_tn(high[:, part], turn_lo[...])
            ).astype(jnp.bfloat16)
            for band in range(bands):
                out_ref[band * tiles + first + inner] = restored[
                    band * local : (band + 1) * local
                ]


def filtered(interferograms, rows_split, side):
    local, full_rows, full_cols = interferograms.shape
    cells = side * side
    tiles = full_cols // side
    tables = spectral_tables(side)
    blocks = interferograms.reshape(local * full_rows, full_cols // 128, 128)
    return pl.pallas_call(
        functools.partial(filter_kernel, local, side),
        out_shape=jax.ShapeDtypeStruct((rows_split * tiles, local, cells), jnp.bfloat16),
        in_specs=[pl.BlockSpec(memory_space=pltpu.HBM)] * 4,
        out_specs=WHOLE,
        scratch_shapes=[
            pltpu.VMEM((cells, tiles * rows_split * local), jnp.float32),
            pltpu.VMEM((full_cols // 128, local * full_rows, 128), jnp.float32),
            pltpu.VMEM((2 * cells, cells), jnp.bfloat16),
            pltpu.VMEM((2 * cells, cells), jnp.bfloat16),
            pltpu.VMEM((cells, cells), jnp.bfloat16),
            pltpu.SemaphoreType.DMA((4,)),
        ],
        compiler_params=pltpu.CompilerParams(vmem_limit_bytes=40 * 1024 * 1024),
        name="filter",
    )(blocks.transpose(1, 0, 2), *tables)


def prepare_kernel(epochs_ref, track_ref, c0_ref, c1_ref, ct0_ref, ct1_ref, perm_ref):
    pairs = track_ref.shape[1]
    ascending = (track_ref[...] == 0).astype(jnp.float32)
    one = jnp.broadcast_to(ascending, (8, pairs)).astype(jnp.bfloat16)
    row_id = lax.broadcasted_iota(jnp.int32, (pairs, pairs), 0)
    col_id = lax.broadcasted_iota(jnp.int32, (pairs, pairs), 1)
    upto = (row_id <= col_id).astype(jnp.float32).astype(jnp.bfloat16)
    count = mm(one, upto)[0:1].astype(jnp.int32)
    place = lax.broadcasted_iota(jnp.int32, (1, pairs), 1)
    position = jnp.where(track_ref[...] == 0, count - 1, ASC + place - count)
    perm = (row_id == position).astype(jnp.float32).astype(jnp.bfloat16)
    perm_ref[...] = perm
    epoch_id = lax.broadcasted_iota(jnp.int32, (NEPOCH, pairs), 0)
    change = (epoch_id == epochs_ref[1:2, :]).astype(jnp.float32) - (
        epoch_id == epochs_ref[0:1, :]
    ).astype(jnp.float32)
    change = change.astype(jnp.bfloat16)
    c0_ref[...] = mm_nt(perm[:ASC], change).astype(jnp.bfloat16)
    c1_ref[...] = mm_nt(perm[ASC:], change).astype(jnp.bfloat16)
    ct0_ref[...] = mm_nt(change, perm[:ASC]).astype(jnp.bfloat16)
    ct1_ref[...] = mm_nt(change, perm[ASC:]).astype(jnp.bfloat16)


def prepare(epochs, track):
    pairs = track.shape[0]
    rest = pairs - ASC
    shapes = ((ASC, NEPOCH), (rest, NEPOCH), (NEPOCH, ASC), (NEPOCH, rest), (pairs, pairs))
    return pl.pallas_call(
        prepare_kernel,
        out_shape=[jax.ShapeDtypeStruct(s, jnp.bfloat16) for s in shapes],
        in_specs=[WHOLE] * 2,
        out_specs=[WHOLE] * 5,
        cost_estimate=pl.CostEstimate(
            flops=6 * pairs * pairs * NEPOCH, bytes_accessed=8 * pairs * pairs, transcendentals=0
        ),
        name="prepare",
    )(epochs.T, track[None, :])


def smoothing_tables(side):
    cells = side * side
    offsets = np.arange(-RADIUS, RADIUS + 1)
    total = np.sum(np.exp(-offsets * offsets / 8.0))

    def tap(distance):
        return np.where(np.abs(distance) <= RADIUS, np.exp(-distance * distance / 8.0) / total, 0.0)

    cell = np.arange(cells)
    row, col = cell // side, cell % side
    inner = np.arange(side * RADIUS)
    own, strips, picks = [], [], []
    for mine, other, s_mine, s_other in (
        (row, col, inner // side, inner % side),
        (col, row, inner % RADIUS, inner // RADIUS),
    ):
        same = other[:, None] == other[None, :]
        own.append(np.where(same, tap(mine[:, None] - mine[None, :]), 0.0))
        lines = s_other[:, None] == other[None, :]
        for shift in (-RADIUS, side):
            strips.append(np.where(lines, tap(s_mine[:, None] + shift - mine[None, :]), 0.0))
        for first in (0, side - RADIUS):
            hit = (other[:, None] == s_other[None, :]) & (
                mine[:, None] == s_mine[None, :] + first
            )
            picks.append(hit.astype(np.float32).astype(jnp.bfloat16))
    tables = (*split_table(np.stack(own)), *split_table(np.stack(strips)), np.stack(picks))
    return [jnp.asarray(table) for table in tables]


def invert_kernel(
    obs_ref, mask_ref, c0_ref, c1_ref, ct0_ref, ct1_ref, perm_ref,
    own_hi, own_lo, strip_hi, strip_lo, pick_ref,
    out_ref, meas_ref, weight_ref, send_buf, recv_buf, send_sem, recv_sem,
):
    design = (c0_ref, c1_ref)
    transposed = (ct0_ref, ct1_ref)
    spans = (slice(0, ASC), slice(ASC, obs_ref.shape[0]))
    me = {name: lax.axis_index(name) for name in ("pair", "tile")}
    size = {name: lax.axis_size(name) for name in ("pair", "tile")}
    axes = ("pair", "tile")

    def there(axis, step):
        return {"pair": me["pair"], "tile": me["tile"], axis: me[axis] + step}

    def target(axis, step):
        where = there(axis, step)
        return (where["pair"], where["tile"])

    def has(axis, step):
        return me[axis] > 0 if step < 0 else me[axis] < size[axis] - 1

    recv_buf[...] = jnp.zeros_like(recv_buf)
    barrier = pltpu.get_barrier_semaphore()
    for axis in axes:
        for step in (-1, 1):

            @pl.when(has(axis, step))
            def _():
                pl.semaphore_signal(
                    barrier, inc=1, device_id=target(axis, step), device_id_type=MESH
                )

    meas_ref[...] = mm(perm_ref[...], obs_ref[...])
    out_ref[...] = jnp.zeros_like(out_ref)

    peers = sum(
        jnp.where(has(axis, step), 1, 0) for axis in axes for step in (-1, 1)
    )
    pl.semaphore_wait(barrier, peers)

    def forward(field, track, passes):
        mixed = UP_COEF[track] * field[:NEPOCH] + EAST_COEF[track] * field[NEPOCH:]
        high, low = halves(mixed)
        result = mm(design[track][...], high)
        if passes > 1:
            result = result + mm(design[track][...], low)
        return result

    def backward(parts):
        sums = []
        for track in (0, 1):
            high, low = halves(parts[track])
            sums.append(mm(transposed[track][...], high) + mm(transposed[track][...], low))
        return jnp.concatenate(
            [
                UP_COEF[0] * sums[0] + UP_COEF[1] * sums[1],
                EAST_COEF[0] * sums[0] + EAST_COEF[1] * sums[1],
            ],
            axis=0,
        )

    def total(value):
        return jnp.sum(value, axis=0, keepdims=True)

    def exchange(turn, which, field_hi):
        axis = axes[which]
        copies = []
        for side, step in ((0, -1), (1, 1)):
            slot = 2 * which + side
            edge = mm(field_hi, pick_ref[slot])
            send_buf[turn, slot] = jnp.concatenate(
                [edge[:NEPOCH], edge[NEPOCH:]], axis=1
            ).astype(jnp.bfloat16)
            landing = 2 * which + 1 - side
            copy = pltpu.make_async_remote_copy(
                src_ref=send_buf.at[turn, slot],
                dst_ref=recv_buf.at[turn, landing],
                send_sem=send_sem.at[turn, slot],
                recv_sem=recv_sem.at[turn, landing],
                device_id=target(axis, step),
                device_id_type=MESH,
            )

            @pl.when(has(axis, step))
            def _():
                copy.start()

            copies.append((copy, axis, step, slot))
        return copies

    def smooth_own(which, high, low):
        return mm(high, own_hi[which]) + mm(high, own_lo[which]) + mm(low, own_hi[which])

    def finish(turn, which, copies):
        for copy, axis, step, slot in copies:
            incoming = pltpu.make_async_remote_copy(
                src_ref=send_buf.at[turn, slot],
                dst_ref=recv_buf.at[turn, slot],
                send_sem=send_sem.at[turn, slot],
                recv_sem=recv_sem.at[turn, slot],
                device_id=target(axis, step),
                device_id_type=MESH,
            )

            @pl.when(has(axis, step))
            def _():
                copy.wait_send()
                incoming.wait_recv()

        parts = []
        for part in (0, 1):
            value = 0.0
            for side in (0, 1):
                slot = 2 * which + side
                width = strip_hi.shape[1]
                edge = recv_buf[turn, slot, :, part * width : (part + 1) * width]
                value = value + mm(edge, strip_hi[slot]) + mm(edge, strip_lo[slot])
            parts.append(value)
        return jnp.concatenate(parts, axis=0)

    def one_round(turn, carry):
        solution = out_ref[...]
        pulls = []
        for track in (0, 1):
            misfit = meas_ref[spans[track]] - forward(solution, track, 2)
            weight = mask_ref[track : track + 1] * HUBER_EDGE / jnp.maximum(
                jnp.abs(misfit), HUBER_EDGE
            )
            weight_ref[spans[track]] = weight
            pulls.append(weight * misfit)
        residual = backward(pulls) - TIKHONOV * solution
        norm = total(residual * residual)
        pulls, curve = [], TIKHONOV * norm
        for track in (0, 1):
            image = forward(residual, track, 2)
            pull = weight_ref[spans[track]] * image
            curve = curve + total(pull * image)
            pulls.append(pull)
        step_len = norm / (curve + EPSILON)
        solution = solution + step_len * residual
        after = residual - step_len * (backward(pulls) + TIKHONOV * residual)
        norm_next = total(after * after)
        direction = after + norm_next / (norm + EPSILON) * residual
        curve = TIKHONOV * total(direction * direction)
        for track in (0, 1):
            image = forward(direction, track, 1)
            curve = curve + total(weight_ref[spans[track]] * image * image)
        solution = solution + norm_next / (curve + EPSILON) * direction
        for which in (0, 1):
            high, low = halves(solution)
            copies = exchange(turn, which, high)
            solution = smooth_own(which, high, low)
            solution = solution + finish(turn, which, copies)
        out_ref[...] = solution
        return carry

    lax.fori_loop(0, ROUNDS, one_round, 0)


def invert(observed, mask_cells, epochs, track, side):
    pairs, cells = observed.shape
    strip = 2 * side * RADIUS
    tables = smoothing_tables(side)
    return pl.pallas_call(
        invert_kernel,
        out_shape=jax.ShapeDtypeStruct((2 * NEPOCH, cells), jnp.float32),
        in_specs=[WHOLE] * 12,
        out_specs=WHOLE,
        scratch_shapes=[
            pltpu.VMEM((pairs, cells), jnp.float32),
            pltpu.VMEM((pairs, cells), jnp.float32),
            pltpu.VMEM((ROUNDS, 4, NEPOCH, strip), jnp.bfloat16),
            pltpu.VMEM((ROUNDS, 4, NEPOCH, strip), jnp.bfloat16),
            pltpu.SemaphoreType.DMA((ROUNDS, 4)),
            pltpu.SemaphoreType.DMA((ROUNDS, 4)),
        ],
        compiler_params=pltpu.CompilerParams(
            collective_id=0, has_side_effects=True, vmem_limit_bytes=60 * 1024 * 1024
        ),
        name="invert",
    )(observed, mask_cells, *prepare(epochs, track), *tables)


def per_device(interferograms, coherence, epochs, track):
    rows_split = lax.axis_size("pair")
    local_pairs, full_rows, full_cols = interferograms.shape
    patch_len = full_rows // rows_split
    cell_count = patch_len * patch_len
    cleaned = filtered(interferograms, rows_split, patch_len)
    received = lax.all_to_all(
        cleaned,
        ("pair", "tile"),
        split_axis=0,
        concat_axis=0,
        tiled=True,
    )
    observed = received.reshape(-1, cell_count)
    mask_cells = coherence.reshape(2, cell_count).astype(jnp.float32)

    solution = invert(observed, mask_cells, epochs, track, patch_len)
    return solution.reshape(2, NEPOCH, patch_len, patch_len)


def solution(mesh):
    placed = (P(("pair", "tile"), None, None), P(None, "pair", "tile"), P(), P())
    return jax.shard_map(
        per_device,
        mesh=mesh,
        in_specs=placed,
        out_specs=P(None, None, "pair", "tile"),
        check_vma=False,
    )
```
